32 devices in a mesh: groups: 2 (over x), seq: 8 (over z, y), sub: 2 (over core).
Axes of the slice: x: 2, y: 2, z: 4, core: 2. Of those that a mesh axis runs over, the one named last changes fastest.
Arguments:
- frames: bfloat16 [2048, 1024], P(('groups', 'seq', 'sub')), parts along dimension 0, may hold values from -6 to 6
- fine_gain: float32 [1024], replicated, may hold values from 0.1 to 1.9
- dw_kernel: bfloat16 [5, 1024], replicated, may hold values from -3 to 3
- w_down: bfloat16 [4096, 4096], P(None, 'seq'), may hold values from -0.21875 to 0.21875
- coarse_gain: float32 [4096], replicated, may hold values from 0.1 to 1.9
- w_qkv: bfloat16 [3, 4096, 4096], P(None, None, 'seq'), may hold values from -1.609375 to 1.609375
- w_out: bfloat16 [4096, 4096], P('seq'), may hold values from -0.09375 to 0.09375
- w_up: bfloat16 [4096, 4096], P('seq'), may hold values from -0.09375 to 0.09375
Outputs:
- denoised: bfloat16 [2048, 1024], P(('groups', 'seq', 'sub')), parts along dimension 0
The draws below stay inside these ranges and needn't reach their ends.
There are 2 independent parts, one for each index of `groups`. The reference program is written for one: setup_inputs(seed, part) draws one part's arguments, and reference() takes and returns one part's arrays. A program takes and returns all parts, laid end to end along the dimension named above; an argument that names none is the same for every part. Nothing has to cross between parts.
All inputs are finite; a program needn't handle non-finite values.
Results may differ from the reference program's by a relative error of at most 0.012.
Values may be sent and summed in bfloat16 or wider, within the bound.
No kernel may reach another device: no remote copies, remote signals or barrier semaphores. Data moves between devices by JAX's collectives and lax.ppermute only.
A program may use at most 128 MiB of HBM per device.

```python
import math
import jax
import jax.numpy as jnp
from jax import lax

DF = 1024
DC = 4096
H = 32
HD = 128
KW = 5
FRAMES = 1024
NC = 256


def draw_w_down(key, part):
    key_base, key_cols = jax.random.split(key)
    basic = jax.random.truncated_normal(key_base, -6.0, 6.0, (4 * DF, DC), jnp.float32)
    jitter = jax.random.uniform(key_cols, (DC,), jnp.float32)
    levels = (jnp.arange(DC, dtype=jnp.float32) + jitter) / DC
    return (basic * (0.22 * jnp.exp(2.302585 * levels) / math.sqrt(4 * DF))).astype(jnp.bfloat16)


def draw_w_qkv(key, part):
    key_base = jax.random.fold_in(key, 0)
    basic = jax.random.truncated_normal(key_base, -6.0, 6.0, (3, DC, H * HD), jnp.float32)
    factor = 1.0 / math.sqrt(DC)
    key_part = basic[1] * (1.41421 * factor)
    value_part = basic[2] * factor
    query_part = basic[0] * (1.41421 * factor)
    return jnp.stack([query_part, key_part, value_part]).astype(jnp.bfloat16)


def level_of(rng, dims, pieces, smallest, largest):
    gain, own = 1.0, jax.random.fold_in(rng, 6)
    for position, blocks in pieces:
        draws = jnp.exp(jax.random.uniform(jax.random.fold_in(own, position), (blocks,), jnp.float32, smallest / len(pieces), largest / len(pieces)))
        gain = gain * jnp.repeat(draws, dims[position] // blocks).reshape([-1 if axis == position else 1 for axis in range(len(dims))])
    return gain


def gaussian(stream_key, dims, deviation, limit, pieces=(), kind=jnp.bfloat16):
    factor_of = level_of(stream_key, dims, pieces, -0.22, 0.18) if pieces else 1.0
    array = jax.random.normal(stream_key, dims, jnp.float32) * deviation * factor_of
    return jnp.minimum(jnp.maximum(array, -limit), limit).astype(kind)


def setup_inputs(seed: int = 0, part: int = 0) -> dict:
    key_of = jax.random.split(jax.random.key(seed), 9)
    part_splits = jax.random.split(jax.random.fold_in(key_of[8], part), 9)
    return {
        "frames": gaussian(part_splits[0], (FRAMES, DF), 1.0, 6.0, ((0, 16),)),
        "fine_gain": jnp.clip(1.0 + 0.18 * jax.random.normal(key_of[1], (DF,), jnp.float32), 0.1, 1.9),
        "dw_kernel": gaussian(key_of[2], (KW, DF), 0.5, 3.0),
        "w_down": draw_w_down(jax.random.fold_in(key_of[8], 71), part),
        "coarse_gain": jnp.clip(1.0 + 0.18 * jax.random.normal(key_of[4], (DC,), jnp.float32), 0.1, 1.9),
        "w_qkv": draw_w_qkv(jax.random.fold_in(key_of[8], 71), part),
        "w_out": gaussian(key_of[6], (H * HD, DC), (H * HD) ** -0.5, 0.09375, ((0, 8),)),
        "w_up": gaussian(key_of[7], (DC, 4 * DF), DC ** -0.5, 0.09375, ((0, 8),)),
    }


epsilon = 1e-06

def reference(frames, fine_gain, dw_kernel, w_down, coarse_gain, w_qkv, w_out, w_up):
    frames_f32 = frames.astype(jnp.float32)
    normed_fine = (frames_f32 * lax.rsqrt(lax.optimization_barrier(jnp.mean(frames_f32 * frames_f32, axis=1, keepdims=True)) + epsilon) * fine_gain.astype(jnp.float32)).astype(jnp.bfloat16)
    half_width = KW // 2
    padded = jnp.pad(normed_fine, ((half_width, half_width), (0, 0)))
    convolved = jnp.zeros((FRAMES, DF), jnp.float32)
    for offset in range(KW):
        convolved = convolved + padded[offset:offset + FRAMES].astype(jnp.float32) * dw_kernel[offset].astype(jnp.float32)
    patches = convolved.astype(jnp.bfloat16).reshape(NC, 4 * DF)
    coarse = jnp.dot(patches, w_down, preferred_element_type=jnp.float32).astype(jnp.bfloat16)
    coarse_f32 = coarse.astype(jnp.float32)
    normed_coarse = (coarse_f32 * lax.rsqrt(lax.optimization_barrier(jnp.mean(coarse_f32 * coarse_f32, axis=1, keepdims=True)) + epsilon) * coarse_gain.astype(jnp.float32)).astype(jnp.bfloat16)
    queries = jnp.dot(normed_coarse, w_qkv[0], preferred_element_type=jnp.float32).astype(jnp.bfloat16)
    keys_all = jnp.dot(normed_coarse, w_qkv[1], preferred_element_type=jnp.float32).astype(jnp.bfloat16)
    values_all = jnp.dot(normed_coarse, w_qkv[2], preferred_element_type=jnp.float32).astype(jnp.bfloat16)
    query_heads = queries.reshape(NC, H, HD).transpose(1, 0, 2)
    key_heads = keys_all.reshape(NC, H, HD).transpose(1, 0, 2)
    value_heads = values_all.reshape(NC, H, HD).transpose(1, 0, 2)
    score_scale = 1.0 / math.sqrt(HD)

    def one_head(operands):
        query_one, key_one, value_one = operands
        scores = jnp.dot(query_one, key_one.T, preferred_element_type=jnp.float32) * score_scale
        peak = lax.optimization_barrier(jnp.max(scores, axis=1, keepdims=True))
        weights = jnp.exp(scores - peak)
        weights = (weights / lax.optimization_barrier(jnp.sum(weights, axis=1, keepdims=True))).astype(jnp.bfloat16)
        return jnp.dot(weights, value_one, preferred_element_type=jnp.float32).astype(jnp.bfloat16)
    attended = lax.map(one_head, (query_heads, key_heads, value_heads))
    attended = attended.transpose(1, 0, 2).reshape(NC, H * HD)
    projected = jnp.dot(attended, w_out, preferred_element_type=jnp.float32)
    mixed = (coarse_f32 + projected).astype(jnp.bfloat16)
    lifted = jnp.dot(mixed, w_up, preferred_element_type=jnp.float32).reshape(FRAMES, DF)
    return (frames_f32 + lifted).astype(jnp.bfloat16)
```

```python
import math

import jax
import jax.numpy as jnp
from jax import lax
from jax.sharding import PartitionSpec as P

DF = 1024
HD = 128
KW = 5


epsilon = 1e-06


def padded_2(array, sides, width):
    for axis, dim in sides:
        size, length = (lax.axis_size(axis), array.shape[dim])
        up = [(i, (i + 1) % size) for i in range(size - 1)]
        down = [(j, i) for i, j in up]
        last = lax.slice_in_dim(array, length - width, length, axis=dim)
        leading = lax.slice_in_dim(array, 0, width, axis=dim)
        before = lax.ppermute(last, axis, up)
        after = lax.ppermute(leading, axis, down)
        array = jnp.concatenate([before, array, after], axis=dim)
    return array


def flip(value, axis, mask):
    pairs = [(source, source ^ mask) for source in range(lax.axis_size(axis))]
    return lax.ppermute(value, axis, pairs)


def relayed(mask, size):
    return mask & 1 == 1 and mask >= max(size // 2, 2)


def gather_flips(value, axis):
    size = lax.axis_size(axis)
    blocks = [value] + [None] * (size - 1)
    order = sorted(range(1, size), reverse=True)
    for mask in order:
        if not relayed(mask, size):
            blocks[mask] = flip(value, axis, mask)
    for mask in order:
        if relayed(mask, size):
            blocks[mask] = flip(blocks[mask ^ 1], axis, 1)
    return blocks


def scatter_flips(chunk_of, axis):
    size = lax.axis_size(axis)
    order = sorted(range(1, size), reverse=True)
    passed = {}
    for mask in order:
        if relayed(mask, size):
            passed[mask ^ 1] = flip(chunk_of(mask).astype(jnp.bfloat16), axis, 1)
    total = chunk_of(0)
    arrived = []
    for mask in order:
        if not relayed(mask, size):
            chunk = chunk_of(mask)
            if mask in passed:
                chunk = chunk + passed[mask].astype(jnp.float32)
            arrived.append(flip(chunk.astype(jnp.bfloat16), axis, mask))
    for value in arrived:
        total = total + value.astype(jnp.float32)
    return total


def in_index_order(stacked, axis):
    me, size = lax.axis_index(axis), lax.axis_size(axis)
    bit = 1
    while bit < size:
        shape = stacked.shape
        split = stacked.reshape((size // (2 * bit), 2, bit) + shape[1:])
        stacked = jnp.where((me & bit) != 0, split[:, ::-1], split).reshape(shape)
        bit *= 2
    return stacked


def attend(queries, keys_all, values_all, heads_here):
    row_total = queries.shape[0]
    query_heads = queries.reshape(row_total, heads_here, HD)
    key_heads = keys_all.reshape(keys_all.shape[0], heads_here, HD)
    value_heads = values_all.reshape(values_all.shape[0], heads_here, HD)
    scores = jnp.einsum(
        "qhd,khd->hqk", query_heads, key_heads, preferred_element_type=jnp.float32
    ) * (1.0 / math.sqrt(HD))
    peak = jnp.max(scores, axis=2, keepdims=True)
    weights = jnp.exp(scores - peak)
    weights = (weights / jnp.sum(weights, axis=2, keepdims=True)).astype(jnp.bfloat16)
    return (
        jnp.einsum("hqk,khd->qhd", weights, value_heads, preferred_element_type=jnp.float32)
        .astype(jnp.bfloat16)
        .reshape(row_total, heads_here * HD)
    )


def per_device(frames, fine_gain, dw_kernel, w_down, coarse_gain, w_qkv, w_out, w_up):
    frame_rows = frames.shape[0]
    columns = w_qkv.shape[2]
    heads_here = columns // HD
    me, size = lax.axis_index("seq"), lax.axis_size("seq")
    frames_f32 = frames.astype(jnp.float32)
    normed_fine = (
        frames_f32
        * lax.rsqrt(jnp.mean(frames_f32 * frames_f32, axis=1, keepdims=True) + epsilon)
        * fine_gain
    ).astype(jnp.bfloat16)
    padded = padded_2(normed_fine, ((("seq", "sub"), 0),), KW // 2)
    convolved = jnp.zeros((frame_rows, DF), jnp.float32)
    for offset in range(KW):
        convolved = convolved + padded[offset : offset + frame_rows].astype(
            jnp.float32
        ) * dw_kernel[offset].astype(jnp.float32)
    own_tokens = frame_rows // 4
    tokens = own_tokens * size
    patches = convolved.astype(jnp.bfloat16).reshape(own_tokens, 4 * DF)
    all_patches = jnp.concatenate(gather_flips(patches, "seq"), axis=0)
    coarse = jnp.dot(all_patches, w_down, preferred_element_type=jnp.float32).astype(jnp.bfloat16)
    coarse = in_index_order(coarse.reshape(size, own_tokens, columns), "seq").reshape(
        tokens, columns
    )

    coarse_f32 = coarse.astype(jnp.float32)
    blocks = gather_flips(coarse, "seq")
    squares = jnp.zeros((tokens, 1), jnp.float32)
    products = [jnp.zeros((tokens, columns), jnp.float32) for _ in range(3)]
    for mask in sorted(range(size), key=lambda m: (relayed(m, size), m)):
        start = (me ^ mask) * columns
        block = blocks[mask].astype(jnp.float32)
        squares = squares + jnp.sum(block * block, axis=1, keepdims=True)
        gained = (block * lax.dynamic_slice_in_dim(coarse_gain, start, columns)).astype(jnp.bfloat16)
        for which in range(3):
            piece = lax.dynamic_slice(w_qkv, (which, start, 0), (1, columns, columns))[0]
            products[which] = products[which] + jnp.dot(
                gained, piece, preferred_element_type=jnp.float32
            )
    scale = lax.rsqrt(squares / (columns * size) + epsilon)
    queries, own_keys, own_values = [(p * scale).astype(jnp.bfloat16) for p in products]
    other_keys, other_values = flip(own_keys, "sub", 1), flip(own_values, "sub", 1)
    keys_all = jnp.concatenate([own_keys, other_keys], axis=0)
    values_all = jnp.concatenate([own_values, other_values], axis=0)
    attended = attend(queries, keys_all, values_all, heads_here)

    def out_chunk(mask):
        piece = lax.dynamic_slice_in_dim(w_out, (me ^ mask) * columns, columns, axis=1)
        return jnp.dot(attended, piece, preferred_element_type=jnp.float32)

    mixed = (coarse_f32 + scatter_flips(out_chunk, "seq")).astype(jnp.bfloat16)
    lifted_part = jnp.dot(mixed, w_up, preferred_element_type=jnp.float32)

    def up_chunk(mask):
        return lax.dynamic_slice_in_dim(lifted_part, (me ^ mask) * own_tokens, own_tokens, axis=0)

    lifted = scatter_flips(up_chunk, "seq")
    return (frames_f32 + lifted.reshape(frame_rows, DF)).astype(jnp.bfloat16)


def solution(mesh):
    placed = (
        P(("groups", "seq", "sub"), None),
        P(),
        P(),
        P(None, "seq"),
        P(),
        P(None, None, "seq"),
        P("seq", None),
        P("seq", None),
    )
    return jax.shard_map(
        per_device,
        mesh=mesh,
        in_specs=placed,
        out_specs=P(("groups", "seq", "sub"), None),
        check_vma=False,
    )
```

```python
import functools
import math

import jax
import jax.numpy as jnp
from jax import lax
from jax.experimental import pallas as pl
from jax.experimental.pallas import tpu as pltpu
from jax.sharding import PartitionSpec as P

DF = 1024
HD = 128
KW = 5
VMEM = pltpu.VMEM


epsilon = 1e-06


def flip(value, axis, mask):
    pairs = [(source, source ^ mask) for source in range(lax.axis_size(axis))]
    return lax.ppermute(value, axis, pairs)


def relayed(mask, size):
    return mask & 1 == 1 and mask >= max(size // 2, 2)


def far_first(size):
    return sorted(range(1, size), reverse=True)


def gather_flips(value, axis):
    size = lax.axis_size(axis)
    blocks = [value] + [None] * (size - 1)
    for mask in far_first(size):
        if not relayed(mask, size):
            blocks[mask] = flip(value, axis, mask)
    for mask in far_first(size):
        if relayed(mask, size):
            blocks[mask] = flip(blocks[mask ^ 1], axis, 1)
    return blocks


def scatter_flips(relay_chunks, direct_chunks, axis):
    size = lax.axis_size(axis)
    passed = {mask ^ 1: flip(chunk, axis, 1) for mask, chunk in relay_chunks.items()}
    arrived = []
    for mask in far_first(size):
        if mask in direct_chunks:
            chunk = direct_chunks[mask]
            if mask in passed:
                chunk = (chunk + passed[mask].astype(jnp.float32)).astype(jnp.bfloat16)
            arrived.append(flip(chunk, axis, mask))
    return arrived


def call(body, outs, scratch, in_memory, *operands):
    specs = [
        pl.BlockSpec(memory_space=pl.ANY if where == "h" else VMEM) for where in in_memory
    ]
    return pl.pallas_call(
        body,
        out_shape=outs,
        in_specs=specs,
        out_specs=jax.tree.map(lambda _: pl.BlockSpec(memory_space=VMEM), outs),
        scratch_shapes=scratch,
        compiler_params=pltpu.CompilerParams(vmem_limit_bytes=48 * 2**20),
    )(*operands)


def sds(shape, dtype):
    return jax.ShapeDtypeStruct(shape, dtype)


def dot(left, right):
    return jnp.dot(left, right, preferred_element_type=jnp.float32)


def offset(mask, width):
    return pl.multiple_of((lax.axis_index("seq") ^ mask) * width, width)


def start_all(copies):
    for copy in copies:
        copy.start()
    return copies


def down_kernel(size, own_tokens, pieces, *refs):
    blocks, w_ref, out_ref, held, sems = refs[:size], *refs[size:]
    depth = w_ref.shape[0] // pieces
    copies = start_all(
        [
            pltpu.make_async_copy(w_ref.at[pl.ds(p * depth, depth)], held.at[p], sems.at[p])
            for p in range(pieces)
        ]
    )
    total = None
    for p in range(pieces):
        rows = jnp.concatenate([b[:, p * depth : (p + 1) * depth] for b in blocks], axis=0)
        copies[p].wait()
        product = dot(rows, held[p])
        total = product if total is None else total + product
    total = total.astype(jnp.bfloat16)
    for mask in range(size):
        out_ref[pl.ds(offset(mask, own_tokens), own_tokens), :] = total[
            mask * own_tokens : (mask + 1) * own_tokens
        ]


def qkv_steps(masks, blocks, gain_ref, w_ref, held, sems, totals, squares):
    columns = blocks[0].shape[1]
    copies = start_all(
        [
            pltpu.make_async_copy(
                w_ref.at[:, pl.ds(offset(mask, columns), columns), :], held.at[i], sems.at[i]
            )
            for i, mask in enumerate(masks)
        ]
    )
    for i, mask in enumerate(masks):
        block = blocks[i][...].astype(jnp.float32)
        part = jnp.sum(block * block, axis=1, keepdims=True)
        squares = part if squares is None else squares + part
        gained = (block * gain_ref[:, pl.ds(offset(mask, columns), columns)]).astype(jnp.bfloat16)
        copies[i].wait()
        products = [dot(gained, held[i, which]) for which in range(3)]
        totals = products if totals is None else [t + p for t, p in zip(totals, products)]
    return totals, squares


def qkv_early(masks, *refs):
    count = len(masks)
    blocks, (gain_ref, w_ref, totals_ref, squares_ref, held, sems) = refs[:count], refs[count:]
    totals, squares = qkv_steps(masks, blocks, gain_ref, w_ref, held, sems, None, None)
    for which in range(3):
        totals_ref[which] = totals[which]
    squares_ref[...] = jnp.broadcast_to(squares, squares_ref.shape)


def qkv_late(masks, features, *refs):
    count = len(masks)
    blocks = refs[:count]
    gain_ref, w_ref, totals_ref, squares_ref, q_ref, kv_ref, held, sems = refs[count:]
    totals, squares = qkv_steps(
        masks,
        blocks,
        gain_ref,
        w_ref,
        held,
        sems,
        [totals_ref[which] for which in range(3)],
        squares_ref[:, :1],
    )
    scale = lax.rsqrt(squares / features + epsilon)
    q_ref[...] = (totals[0] * scale).astype(jnp.bfloat16)
    kv_ref[0] = (totals[1] * scale).astype(jnp.bfloat16)
    kv_ref[1] = (totals[2] * scale).astype(jnp.bfloat16)


def out_copies(masks, columns, w_ref, held, sems):
    return start_all(
        [
            pltpu.make_async_copy(
                w_ref.at[:, pl.ds(offset(mask, columns), columns)], held.at[i], sems.at[i]
            )
            for i, mask in enumerate(masks)
        ]
    )


def attend_kernel(masks, q_ref, own_ref, other_ref, w_ref, *refs):
    attended_ref, chunk_refs, held, sems = refs[0], refs[1:-2], refs[-2], refs[-1]
    columns = q_ref.shape[1]
    copies = out_copies(masks, columns, w_ref, held, sems)
    contract = (((1,), (1,)), ((), ()))
    for head in range(columns // HD):
        here = slice(head * HD, (head + 1) * HD)
        query = q_ref[:, here]
        scores = [
            lax.dot_general(query, kv[0, :, here], contract, preferred_element_type=jnp.float32)
            * (1.0 / math.sqrt(HD))
            for kv in (own_ref, other_ref)
        ]
        peak = jnp.maximum(*[jnp.max(s, axis=1, keepdims=True) for s in scores])
        weights = [jnp.exp(s - peak) for s in scores]
        norm = sum(jnp.sum(w, axis=1, keepdims=True) for w in weights)
        attended_ref[:, here] = sum(
            dot((w / norm).astype(jnp.bfloat16), kv[1, :, here])
            for w, kv in zip(weights, (own_ref, other_ref))
        ).astype(jnp.bfloat16)
    for i, chunk_ref in enumerate(chunk_refs):
        copies[i].wait()
        chunk_ref[...] = dot(attended_ref[...], held[i]).astype(chunk_ref.dtype)


def out_kernel(masks, attended_ref, w_ref, *refs):
    chunk_refs, held, sems = refs[:-2], refs[-2], refs[-1]
    copies = out_copies(masks, attended_ref.shape[1], w_ref, held, sems)
    for i, chunk_ref in enumerate(chunk_refs):
        copies[i].wait()
        chunk_ref[...] = dot(attended_ref[...], held[i]).astype(chunk_ref.dtype)


def up_kernel(size, arrivals, pieces, coarse_ref, own_ref, *refs):
    arrived, w_ref = refs[:arrivals], refs[arrivals]
    chunk_refs, (held, sums, sems) = refs[arrivals + 1 : -3], refs[-3:]
    own_tokens, width = chunk_refs[0].shape[0], w_ref.shape[1] // pieces
    copies = start_all(
        [
            pltpu.make_async_copy(w_ref.at[:, pl.ds(p * width, width)], held.at[p], sems.at[p])
            for p in range(pieces)
        ]
    )
    mixed = own_ref[...]
    for value in arrived:
        mixed = mixed + value[...].astype(jnp.float32)
    mixed = (coarse_ref[...].astype(jnp.float32) + mixed).astype(jnp.bfloat16)
    for p in range(pieces):
        copies[p].wait()
        sums[...] = dot(mixed, held[p])
        for mask, chunk_ref in enumerate(chunk_refs):
            chunk_ref[:, p * width : (p + 1) * width] = sums[
                pl.ds(offset(mask, own_tokens), own_tokens), :
            ].astype(chunk_ref.dtype)


def edge_rows(frames, width):
    size, inner = lax.axis_size("seq"), lax.axis_size("sub")
    position = lax.axis_index("seq") * inner + lax.axis_index("sub")
    total = size * inner
    first, last = frames[:width], frames[-width:]
    even = (position & 1) == 0
    inside = [(i, i ^ 1) for i in range(total)]
    across = [(i, ((i + 1) ^ 1) - 1) for i in range(1, total - 1)]
    near = lax.ppermute(jnp.where(even, last, first), ("seq", "sub"), inside)
    far = lax.ppermute(jnp.where(even, first, last), ("seq", "sub"), across)
    return jnp.where(even, far, near), jnp.where(even, near, far)


def per_device(frames, fine_gain, dw_kernel, w_down, coarse_gain, w_qkv, w_out, w_up):
    frame_rows = frames.shape[0]
    columns = w_qkv.shape[2]
    size = lax.axis_size("seq")
    features = columns * size
    own_tokens = frame_rows // 4
    tokens = own_tokens * size
    bf16, f32 = jnp.bfloat16, jnp.float32
    direct = [m for m in range(1, size) if not relayed(m, size)]
    relay = [m for m in range(1, size) if relayed(m, size)]
    via = [m ^ 1 for m in relay]

    before, after = edge_rows(frames, KW // 2)
    frames_f32 = frames.astype(f32)

    def normed(rows):
        return (
            rows * lax.rsqrt(jnp.mean(rows * rows, axis=1, keepdims=True) + epsilon) * fine_gain
        ).astype(bf16)

    padded = jnp.concatenate(
        [normed(before.astype(f32)), normed(frames_f32), normed(after.astype(f32))], axis=0
    )
    convolved = jnp.zeros((frame_rows, DF), f32)
    for tap in range(KW):
        convolved = convolved + padded[tap : tap + frame_rows].astype(f32) * dw_kernel[tap].astype(
            f32
        )
    patches = convolved.astype(bf16).reshape(own_tokens, 4 * DF)

    pieces = 8
    coarse = call(
        functools.partial(down_kernel, size, own_tokens, pieces),
        sds((tokens, columns), bf16),
        [VMEM((pieces, 4 * DF // pieces, columns), bf16), pltpu.SemaphoreType.DMA((pieces,))],
        "v" * size + "h",
        *gather_flips(patches, "seq"),
        w_down,
    )

    blocks = gather_flips(coarse, "seq")
    gain_row = coarse_gain.reshape(1, features)
    early = [0] + direct

    def weight_scratch(masks):
        count = len(masks)
        return [VMEM((count, 3, columns, columns), bf16), pltpu.SemaphoreType.DMA((count,))]

    totals, squares = call(
        functools.partial(qkv_early, early),
        (sds((3, tokens, columns), f32), sds((tokens, 128), f32)),
        weight_scratch(early),
        "v" * len(early) + "vh",
        *[blocks[m] for m in early],
        gain_row,
        w_qkv,
    )
    queries, own_kv = call(
        functools.partial(qkv_late, relay, features),
        (sds((tokens, columns), bf16), sds((2, tokens, columns), bf16)),
        weight_scratch(relay),
        "v" * len(relay) + "vhvv",
        *[blocks[m] for m in relay],
        gain_row,
        w_qkv,
        totals,
        squares,
    )
    other_kv = flip(own_kv, "sub", 1)

    def out_scratch(masks):
        count = len(masks)
        return [VMEM((count, columns, columns), bf16), pltpu.SemaphoreType.DMA((count,))]

    attended, *relay_chunks = call(
        functools.partial(attend_kernel, relay),
        (sds((tokens, columns), bf16),) * (1 + len(relay)),
        out_scratch(relay),
        "vvvh",
        queries,
        own_kv,
        other_kv,
        w_out,
    )
    rest = via + [m for m in direct if m not in via] + [0]

    def kind(mask):
        return f32 if mask == 0 or mask in via else bf16

    chunks = call(
        functools.partial(out_kernel, rest),
        tuple(sds((tokens, columns), kind(m)) for m in rest),
        out_scratch(rest),
        "vh",
        attended,
        w_out,
    )
    chunks = dict(zip(rest, chunks))
    own_part = chunks.pop(0)
    arrived = scatter_flips(dict(zip(relay, relay_chunks)), chunks, "seq")

    def up_kind(mask):
        return bf16 if mask in relay else kind(mask)

    lifted = call(
        functools.partial(up_kernel, size, len(arrived), pieces),
        tuple(sds((own_tokens, 4 * DF), up_kind(m)) for m in range(size)),
        [
            VMEM((pieces, columns, 4 * DF // pieces), bf16),
            VMEM((tokens, 4 * DF // pieces), f32),
            pltpu.SemaphoreType.DMA((pieces,)),
        ],
        "vv" + "v" * len(arrived) + "h",
        coarse,
        own_part,
        *arrived,
        w_up,
    )
    arrived = scatter_flips(
        {m: lifted[m] for m in relay}, {m: lifted[m] for m in direct}, "seq"
    )
    total = lifted[0]
    for value in arrived:
        total = total + value.astype(f32)
    return (frames_f32 + total.reshape(frame_rows, DF)).astype(bf16)


def solution(mesh):
    placed = (
        P(("groups", "seq", "sub"), None),
        P(),
        P(),
        P(None, "seq"),
        P(),
        P(None, None, "seq"),
        P("seq", None),
        P("seq", None),
    )
    return jax.shard_map(
        per_device,
        mesh=mesh,
        in_specs=placed,
        out_specs=P(("groups", "seq", "sub"), None),
        check_vma=False,
    )
```

```python
import functools
import math

import jax
import jax.numpy as jnp
from jax import lax
from jax.experimental import pallas as pl
from jax.experimental.pallas import tpu as pltpu
from jax.sharding import PartitionSpec as P

DF = 1024
HD = 128
KW = 5
VMEM = pltpu.VMEM


epsilon = 1e-06


def flip(value, axis, mask):
    pairs = [(source, source ^ mask) for source in range(lax.axis_size(axis))]
    return lax.ppermute(value, axis, pairs)


def relayed(mask, size):
    return mask & 1 == 1 and mask >= max(size // 2, 2)


def far_first(size):
    return sorted(range(1, size), reverse=True)


def after_all(values, others):
    return lax.optimization_barrier((tuple(values), tuple(others)))[0]


def gather_flips(value, axis, fetched):
    size, rows = lax.axis_size(axis), value.shape[0]
    arrays = [value] + [None] * (size - 1)
    for mask in far_first(size):
        if not relayed(mask, size):
            arrays[mask] = flip(value, axis, mask)
    for mask in far_first(size):
        if relayed(mask, size):
            arrays[mask] = flip(after_all((arrays[mask ^ 1],), fetched)[0], axis, 1)
    return arrays, {mask: [(mask, 0, rows)] for mask in range(size)}


def late_masks(size):
    return [m for m in range(size) if relayed(m, size)]


def early_masks(size):
    return [m for m in range(size) if m not in late_masks(size)]


def scatter_plan(size, rows):
    relays = [m for m in far_first(size) if relayed(m, size)]
    via = [m ^ 1 for m in relays]
    rest = via + [m for m in far_first(size) if m not in via and m not in relays]
    first = [(m, [(m, 0, rows)], False) for m in relays]
    second = [(m, [(m, 0, rows)], m in via) for m in rest] + [("own", [(0, 0, rows)], True)]
    return first, second


def scatter_flips(parts, axis):
    size, rows = lax.axis_size(axis), parts["own"].shape[0]

    def plus(part, *others):
        return sum([o.astype(jnp.float32) for o in others], part).astype(jnp.bfloat16)

    arrived = []
    passed = {m ^ 1: flip(parts[m], axis, 1) for m in far_first(size) if relayed(m, size)}
    for mask in far_first(size):
        if not relayed(mask, size):
            part = plus(parts[mask], passed[mask]) if mask in passed else parts[mask]
            arrived.append((flip(part, axis, mask), 0, 0, rows))
    return arrived


def call(body, outs, scratch, in_memory, *operands, aliases=None):
    specs = [
        pl.BlockSpec(memory_space=pl.ANY if where == "h" else VMEM) for where in in_memory
    ]
    return pl.pallas_call(
        body,
        out_shape=outs,
        in_specs=specs,
        out_specs=jax.tree.map(lambda _: pl.BlockSpec(memory_space=VMEM), outs),
        scratch_shapes=scratch,
        input_output_aliases=aliases or {},
        compiler_params=pltpu.CompilerParams(vmem_limit_bytes=20 * 2**20),
    )(
        *[
            pltpu.with_memory_space_constraint(o, pltpu.HBM) if where == "h" else o
            for where, o in zip(in_memory, operands)
        ]
    )


def sds(shape, dtype):
    return jax.ShapeDtypeStruct(shape, dtype)


def dot(left, right):
    return jnp.dot(left, right, preferred_element_type=jnp.float32)


def offset(mask, width):
    return pl.multiple_of((lax.axis_index("seq") ^ mask) * width, width)


def start_all(copies):
    for copy in copies:
        copy.start()
    return copies


def rows_of(refs, place):
    parts = [refs[i][first : first + rows] for i, first, rows in place]
    return parts[0] if len(parts) == 1 else jnp.concatenate(parts, axis=0)


def needed(places, masks):
    which = sorted({i for mask in masks for i, _, _ in places[mask]})
    number = {i: n for n, i in enumerate(which)}
    return which, {m: [(number[i], f, r) for i, f, r in places[m]] for m in masks}


def down_rows(places, refs, product, out_ref):
    first = 0
    for mask, place in places.items():
        rows = sum(r for _, _, r in place)
        out_ref[pl.ds(offset(mask, rows), rows), :] = product[first : first + rows].astype(
            jnp.bfloat16
        )
        first += rows


def fetch_kernel(count, *refs):
    sources, targets, sems = refs[:count], refs[count + 1 : -1], refs[-1]
    copies = start_all(
        [
            pltpu.make_async_copy(source, target, sems.at[n])
            for n, (source, target) in enumerate(zip(sources, targets))
        ]
    )
    for copy in copies:
        copy.wait()


def fetch(after, *weights):
    count = len(weights)
    return call(
        functools.partial(fetch_kernel, count),
        tuple(sds(w.shape, w.dtype) for w in weights),
        [pltpu.SemaphoreType.DMA((count,))],
        "h" * count + "v",
        *weights,
        after,
    )


def slice_copy(w_ref, mask, target, sem):
    columns = target.shape[1]
    return pltpu.make_async_copy(
        w_ref.at[:, pl.ds(offset(mask, columns), columns), :], target, sem
    )


def fetch_slices_kernel(masks, w_ref, _, kept_ref, sems):
    copies = start_all(
        [slice_copy(w_ref, m, kept_ref.at[n], sems.at[n]) for n, m in enumerate(masks)]
    )
    for copy in copies:
        copy.wait()


def down_early(places, count, *refs):
    blocks, (w_ref, later_ref, out_ref, kept_ref, sem) = refs[:count], refs[count:]
    copy = pltpu.make_async_copy(later_ref, kept_ref, sem)
    copy.start()
    rows = jnp.concatenate([rows_of(blocks, place) for place in places.values()], axis=0)
    down_rows(places, blocks, dot(rows, w_ref[...]), out_ref)
    copy.wait()


def down_late(places, count, *refs):
    blocks, w_ref, _, out_ref = refs[:count], *refs[count:]
    rows = jnp.concatenate([rows_of(blocks, place) for place in places.values()], axis=0)
    down_rows(places, blocks, dot(rows, w_ref[...]), out_ref)


def qkv_steps(places, blocks, gain_ref, weights, totals, squares):
    for step, (mask, place) in enumerate(places.items()):
        block = rows_of(blocks, place).astype(jnp.float32)
        columns = block.shape[1]
        part = jnp.sum(block * block, axis=1, keepdims=True)
        squares = part if squares is None else squares + part
        gained = (block * gain_ref[:, pl.ds(offset(mask, columns), columns)]).astype(jnp.bfloat16)
        held = weights(step)
        products = [dot(gained, held[which]) for which in range(3)]
        totals = products if totals is None else [t + p for t, p in zip(totals, products)]
    return totals, squares


def qkv_early(places, kept_masks, count, *refs):
    blocks, (gain_ref, w_ref, kept_ref, totals_ref, squares_ref, held, sems) = (
        refs[:count],
        refs[count:],
    )
    order = list(places)
    streamed = [m for m in order if m not in kept_masks]
    copies = start_all(
        [slice_copy(w_ref, m, held.at[n], sems.at[n]) for n, m in enumerate(streamed)]
    )

    def weights(step):
        mask = order[step]
        if mask in kept_masks:
            return kept_ref.at[kept_masks.index(mask)]
        copies[streamed.index(mask)].wait()
        return held.at[streamed.index(mask)]

    totals, squares = qkv_steps(places, blocks, gain_ref, weights, None, None)
    for which in range(3):
        totals_ref[which] = totals[which]
    squares_ref[...] = jnp.broadcast_to(squares, squares_ref.shape)


def qkv_late(places, features, count, *refs):
    blocks = refs[:count]
    gain_ref, kept_ref, totals_ref, squares_ref, q_ref, kv_ref = refs[count:]
    totals, squares = qkv_steps(
        places,
        blocks,
        gain_ref,
        lambda step: kept_ref.at[step],
        [totals_ref[which] for which in range(3)],
        squares_ref[:, :1],
    )
    scale = lax.rsqrt(squares / features + epsilon)
    q_ref[...] = (totals[0] * scale).astype(jnp.bfloat16)
    kv_ref[0] = (totals[1] * scale).astype(jnp.bfloat16)
    kv_ref[1] = (totals[2] * scale).astype(jnp.bfloat16)


def write_chunks(plan, attended_ref, w_ref, out_refs):
    columns = attended_ref.shape[1]
    for mask in dict.fromkeys(m for _, parts, _ in plan for m, _, _ in parts):
        chunk = dot(attended_ref[...], w_ref[:, pl.ds(offset(mask, columns), columns)])
        write_parts(plan, mask, lambda first, last: chunk[first:last], out_refs, slice(None))


def write_parts(plan, mask, rows, out_refs, columns):
    for (_, parts, _), ref in zip(plan, out_refs):
        at = 0
        for m, first, last in parts:
            if m == mask:
                ref[at : at + last - first, columns] = rows(first, last).astype(ref.dtype)
            at += last - first


def attend_kernel(plan, q_ref, own_ref, other_ref, w_ref, attended_ref, *out_refs):
    columns = q_ref.shape[1]
    contract = (((1,), (1,)), ((), ()))
    for head in range(columns // HD):
        here = slice(head * HD, (head + 1) * HD)
        query = q_ref[:, here]
        scores = [
            lax.dot_general(query, kv[0, :, here], contract, preferred_element_type=jnp.float32)
            * (1.0 / math.sqrt(HD))
            for kv in (own_ref, other_ref)
        ]
        peak = jnp.maximum(*[jnp.max(s, axis=1, keepdims=True) for s in scores])
        weights = [jnp.exp(s - peak) for s in scores]
        norm = sum(jnp.sum(w, axis=1, keepdims=True) for w in weights)
        attended_ref[:, here] = sum(
            dot((w / norm).astype(jnp.bfloat16), kv[1, :, here])
            for w, kv in zip(weights, (own_ref, other_ref))
        ).astype(jnp.bfloat16)
    write_chunks(plan, attended_ref, w_ref, out_refs)


def out_kernel(plan, attended_ref, w_ref, *out_refs):
    write_chunks(plan, attended_ref, w_ref, out_refs)


def up_kernel(size, plan, places, pieces, coarse_ref, own_ref, *refs):
    count = len(places)
    arrived, w_ref, out_refs, (mixed_ref, sums) = (
        refs[:count],
        refs[count],
        refs[count + 1 : -2],
        refs[-2:],
    )
    width = w_ref.shape[1] // pieces
    mixed_ref[...] = own_ref[...]
    for value, (source, target, rows) in zip(arrived, places):
        mixed_ref[target : target + rows, :] += value[source : source + rows].astype(jnp.float32)
    mixed = (coarse_ref[...].astype(jnp.float32) + mixed_ref[...]).astype(jnp.bfloat16)
    own_tokens = mixed.shape[0] // size
    for p in range(pieces):
        here = slice(p * width, (p + 1) * width)
        sums[...] = dot(mixed, w_ref[:, here])
        for mask in range(size):
            chunk = sums[pl.ds(offset(mask, own_tokens), own_tokens), :]
            write_parts(plan, mask, lambda first, last: chunk[first:last], out_refs, here)


def scaled(rows, gain):
    mean = jnp.mean(rows * rows, axis=1, keepdims=True)
    return (rows * lax.rsqrt(mean + epsilon) * gain).astype(jnp.bfloat16).astype(jnp.float32)


def norm_kernel(frames_ref, gain_ref, taps_ref, normed_ref, kept_ref, wide_ref, held, taps, sems):
    copies = start_all(
        [
            pltpu.make_async_copy(source, target, sems.at[n])
            for n, (source, target) in enumerate(
                [(frames_ref, held), (gain_ref, kept_ref), (taps_ref, taps)]
            )
        ]
    )
    for copy in copies:
        copy.wait()
    wide_ref[...] = taps[...].astype(jnp.float32)
    normed_ref[...] = scaled(held[...].astype(jnp.float32), kept_ref[...])


def conv_kernel(before_ref, after_ref, normed_ref, gain_ref, taps_ref, out_ref, padded):
    frame_rows = normed_ref.shape[0]
    edge = KW // 2
    padded[8 - edge : 8, :] = scaled(before_ref[...].astype(jnp.float32), gain_ref[...])
    padded[8 : 8 + frame_rows, :] = normed_ref[...]
    padded[8 + frame_rows : 8 + frame_rows + edge, :] = scaled(
        after_ref[...].astype(jnp.float32), gain_ref[...]
    )
    total = None
    for tap in range(KW):
        first = 8 - edge + tap
        part = padded[first : first + frame_rows, :] * taps_ref[tap : tap + 1, :]
        total = part if total is None else total + part
    out_ref[...] = total.astype(jnp.bfloat16)


def edge_rows(frames, width):
    size, inner = lax.axis_size("seq"), lax.axis_size("sub")
    position = lax.axis_index("seq") * inner + lax.axis_index("sub")
    total = size * inner
    first, last = frames[:width], frames[-width:]
    even = (position & 1) == 0
    inside = [(i, i ^ 1) for i in range(total)]
    across = [(i, ((i + 1) ^ 1) - 1) for i in range(1, total - 1)]
    near = lax.ppermute(jnp.where(even, last, first), ("seq", "sub"), inside)
    far = lax.ppermute(jnp.where(even, first, last), ("seq", "sub"), across)
    return jnp.where(even, far, near), jnp.where(even, near, far)


def per_device(frames, fine_gain, dw_kernel, w_down, coarse_gain, w_qkv, w_out, w_up):
    frame_rows = frames.shape[0]
    columns = w_qkv.shape[2]
    size = lax.axis_size("seq")
    features = columns * size
    own_tokens = frame_rows // 4
    tokens = own_tokens * size
    bf16, f32 = jnp.bfloat16, jnp.float32

    before, after = edge_rows(frames, KW // 2)
    frames_f32 = frames.astype(f32)

    normed, gain_kept, taps = call(
        norm_kernel,
        (sds(frames.shape, f32), sds((1, DF), f32), sds(dw_kernel.shape, f32)),
        [VMEM(frames.shape, bf16), VMEM(dw_kernel.shape, bf16), pltpu.SemaphoreType.DMA((3,))],
        "hhh",
        frames,
        fine_gain.reshape(1, DF),
        dw_kernel,
    )
    patches = call(
        conv_kernel,
        sds(frames.shape, bf16),
        [VMEM((frame_rows + 16, DF), f32)],
        "vvvvv",
        before,
        after,
        normed,
        gain_kept,
        taps,
    ).reshape(own_tokens, 4 * DF)

    pieces = 8
    early, late = early_masks(size), late_masks(size)

    w_down_kept, w_out_kept = fetch(patches, w_down, w_out)
    arrays, places = gather_flips(patches, "seq", (w_down_kept, w_out_kept))
    which, here = needed(places, early)
    coarse, w_up_kept = call(
        functools.partial(down_early, here, len(which)),
        (sds((tokens, columns), bf16), sds(w_up.shape, bf16)),
        [pltpu.SemaphoreType.DMA],
        "v" * len(which) + "vh",
        *[arrays[i] for i in which],
        w_down_kept,
        w_up,
    )
    which, here = needed(places, late)
    coarse = call(
        functools.partial(down_late, here, len(which)),
        sds((tokens, columns), bf16),
        [],
        "v" * len(which) + "vv",
        *[arrays[i] for i in which],
        w_down_kept,
        coarse,
        aliases={len(which) + 1: 0},
    )

    kept_masks = late + early[: len(early) // 2]
    streamed = [m for m in early if m not in kept_masks]
    kept = call(
        functools.partial(fetch_slices_kernel, kept_masks),
        sds((len(kept_masks), 3, columns, columns), bf16),
        [pltpu.SemaphoreType.DMA((len(kept_masks),))],
        "hv",
        w_qkv,
        coarse,
    )
    arrays, places = gather_flips(coarse, "seq", (kept,))
    gain_row = coarse_gain.reshape(1, features)
    which, here = needed(places, early)
    totals, squares = call(
        functools.partial(qkv_early, here, kept_masks, len(which)),
        (sds((3, tokens, columns), f32), sds((tokens, 128), f32)),
        [
            VMEM((len(streamed), 3, columns, columns), bf16),
            pltpu.SemaphoreType.DMA((len(streamed),)),
        ],
        "v" * len(which) + "vhv",
        *[arrays[i] for i in which],
        gain_row,
        w_qkv,
        kept,
    )
    which, here = needed(places, late)
    queries, own_kv = call(
        functools.partial(qkv_late, here, features, len(which)),
        (sds((tokens, columns), bf16), sds((2, tokens, columns), bf16)),
        [],
        "v" * len(which) + "vvvv",
        *[arrays[i] for i in which],
        gain_row,
        kept,
        totals,
        squares,
    )
    other_kv = flip(own_kv, "sub", 1)

    def planned(plan, width):
        return tuple(
            sds((sum(last - first for _, first, last in parts), width), f32 if wide else bf16)
            for _, parts, wide in plan
        )

    first_plan, second_plan = scatter_plan(size, tokens)
    attended, *first = call(
        functools.partial(attend_kernel, first_plan),
        (sds((tokens, columns), bf16),) + planned(first_plan, columns),
        [],
        "vvvv",
        queries,
        own_kv,
        other_kv,
        w_out_kept,
    )
    second = call(
        functools.partial(out_kernel, second_plan),
        planned(second_plan, columns),
        [],
        "vv",
        attended,
        w_out_kept,
    )
    names = [name for name, _, _ in first_plan + second_plan]
    parts = dict(zip(names, [*first, *second]))
    arrived = scatter_flips(parts, "seq")
    first_plan, second_plan = scatter_plan(size, own_tokens)
    lifted = call(
        functools.partial(
            up_kernel, size, first_plan + second_plan, [a[1:] for a in arrived], pieces
        ),
        planned(first_plan + second_plan, 4 * DF),
        [VMEM((tokens, columns), f32), VMEM((tokens, 4 * DF // pieces), f32)],
        "vv" + "v" * len(arrived) + "v",
        coarse,
        parts["own"],
        *[a[0] for a in arrived],
        w_up_kept,
    )
    parts = dict(zip(names, lifted))
    total = parts["own"]
    for value, source, target, rows in scatter_flips(parts, "seq"):
        value = value[source : source + rows].astype(f32)
        total = total + jnp.pad(value, ((target, own_tokens - target - rows), (0, 0)))
    return (frames_f32 + total.reshape(frame_rows, DF)).astype(bf16)


def solution(mesh):
    placed = (
        P(("groups", "seq", "sub"), None),
        P(),
        P(),
        P(None, "seq"),
        P(),
        P(None, None, "seq"),
        P("seq", None),
        P("seq", None),
    )
    return jax.shard_map(
        per_device,
        mesh=mesh,
        in_specs=placed,
        out_specs=P(("groups", "seq", "sub"), None),
        check_vma=False,
    )
```

```python
import functools
import math

import jax
import jax.numpy as jnp
from jax import lax
from jax.experimental import pallas as pl
from jax.experimental.pallas import tpu as pltpu
from jax.sharding import PartitionSpec as P

DF = 1024
HD = 128
KW = 5
VMEM = pltpu.VMEM


epsilon = 1e-06


def flip(value, axis, mask):
    pairs = [(source, source ^ mask) for source in range(lax.axis_size(axis))]
    return lax.ppermute(value, axis, pairs)


def relayed(mask, size):
    return mask & 1 == 1 and mask >= max(size // 2, 2)


def far_first(size):
    return sorted(range(1, size), reverse=True)


def after_all(values, others):
    return lax.optimization_barrier((tuple(values), tuple(others)))[0]


def gather_flips(value, axis, fetched):
    size, rows = lax.axis_size(axis), value.shape[0]
    arrays = [value] + [None] * (size - 1)
    for mask in far_first(size):
        if not relayed(mask, size):
            arrays[mask] = flip(value, axis, mask)
    near = [arrays[m] for m in range(1, size) if arrays[m] is not None and m == 3]
    for n, mask in enumerate(m for m in far_first(size) if relayed(m, size)):
        ready = (*fetched, *near) if n else fetched
        arrays[mask] = flip(after_all((arrays[mask ^ 1],), ready)[0], axis, 1)
    return arrays, {mask: [(mask, 0, rows)] for mask in range(size)}


def late_masks(size):
    return [m for m in range(size) if relayed(m, size)]


def early_masks(size):
    return [m for m in range(size) if m not in late_masks(size)]


def scatter_plan(size, rows):
    relays = [m for m in far_first(size) if relayed(m, size)]
    via = [m ^ 1 for m in relays]
    rest = via + [m for m in far_first(size) if m not in via and m not in relays]
    first = [(m, [(m, 0, rows)], False) for m in relays]
    second = [(m, [(m, 0, rows)], m in via) for m in rest] + [("own", [(0, 0, rows)], True)]
    return first, second


def scatter_flips(parts, axis):
    size, rows = lax.axis_size(axis), parts["own"].shape[0]

    def plus(part, *others):
        return sum([o.astype(jnp.float32) for o in others], part).astype(jnp.bfloat16)

    passed = {m ^ 1: flip(parts[m], axis, 1) for m in far_first(size) if relayed(m, size)}
    beside = flip(parts[2], axis, 2)
    arrived = [(beside, 0, 0, rows)]
    for mask in far_first(size):
        if mask in passed:
            part = plus(parts[mask], passed[mask])
        elif mask == 2 or relayed(mask, size):
            continue
        else:
            part = after_all((parts[mask],), (beside, *passed.values()))[0]
        arrived.append((flip(part, axis, mask), 0, 0, rows))
    return arrived


def call(body, outs, scratch, in_memory, *operands, aliases=None):
    specs = [
        pl.BlockSpec(memory_space=pl.ANY if where == "h" else VMEM) for where in in_memory
    ]
    return pl.pallas_call(
        body,
        out_shape=outs,
        in_specs=specs,
        out_specs=jax.tree.map(lambda _: pl.BlockSpec(memory_space=VMEM), outs),
        scratch_shapes=scratch,
        input_output_aliases=aliases or {},
        compiler_params=pltpu.CompilerParams(vmem_limit_bytes=20 * 2**20),
    )(
        *[
            pltpu.with_memory_space_constraint(o, pltpu.HBM) if where == "h" else o
            for where, o in zip(in_memory, operands)
        ]
    )


def sds(shape, dtype):
    return jax.ShapeDtypeStruct(shape, dtype)


def dot(left, right):
    return jnp.dot(left, right, preferred_element_type=jnp.float32)


def offset(mask, width):
    return pl.multiple_of((lax.axis_index("seq") ^ mask) * width, width)


def start_all(copies):
    for copy in copies:
        copy.start()
    return copies


def rows_of(refs, place):
    parts = [refs[i][first : first + rows] for i, first, rows in place]
    return parts[0] if len(parts) == 1 else jnp.concatenate(parts, axis=0)


def needed(places, masks):
    which = sorted({i for mask in masks for i, _, _ in places[mask]})
    number = {i: n for n, i in enumerate(which)}
    return which, {m: [(number[i], f, r) for i, f, r in places[m]] for m in masks}


def down_rows(places, refs, product, out_ref):
    first = 0
    for mask, place in places.items():
        rows = sum(r for _, _, r in place)
        out_ref[pl.ds(offset(mask, rows), rows), :] = product[first : first + rows].astype(
            jnp.bfloat16
        )
        first += rows


def fetch_kernel(count, *refs):
    sources, targets, sems = refs[:count], refs[count + 1 : -1], refs[-1]
    copies = start_all(
        [
            pltpu.make_async_copy(source, target, sems.at[n])
            for n, (source, target) in enumerate(zip(sources, targets))
        ]
    )
    for copy in copies:
        copy.wait()


def fetch(after, *weights):
    count = len(weights)
    return call(
        functools.partial(fetch_kernel, count),
        tuple(sds(w.shape, w.dtype) for w in weights),
        [pltpu.SemaphoreType.DMA((count,))],
        "h" * count + "v",
        *weights,
        after,
    )


def slice_copy(w_ref, mask, target, sem):
    columns = target.shape[1]
    return pltpu.make_async_copy(
        w_ref.at[:, pl.ds(offset(mask, columns), columns), :], target, sem
    )


def fetch_slices_kernel(masks, w_ref, _, kept_ref, sems):
    copies = start_all(
        [slice_copy(w_ref, m, kept_ref.at[n], sems.at[n]) for n, m in enumerate(masks)]
    )
    for copy in copies:
        copy.wait()


def down_early(places, count, *refs):
    blocks, (w_ref, later_ref, out_ref, kept_ref, sem) = refs[:count], refs[count:]
    copy = pltpu.make_async_copy(later_ref, kept_ref, sem)
    copy.start()
    rows = jnp.concatenate([rows_of(blocks, place) for place in places.values()], axis=0)
    down_rows(places, blocks, dot(rows, w_ref[...]), out_ref)
    copy.wait()


def down_late(places, count, *refs):
    blocks, w_ref, _, out_ref = refs[:count], *refs[count:]
    rows = jnp.concatenate([rows_of(blocks, place) for place in places.values()], axis=0)
    down_rows(places, blocks, dot(rows, w_ref[...]), out_ref)


def qkv_steps(places, blocks, gain_ref, weights, totals, squares):
    for step, (mask, place) in enumerate(places.items()):
        block = rows_of(blocks, place).astype(jnp.float32)
        columns = block.shape[1]
        part = jnp.sum(block * block, axis=1, keepdims=True)
        squares = part if squares is None else squares + part
        gained = (block * gain_ref[:, pl.ds(offset(mask, columns), columns)]).astype(jnp.bfloat16)
        held = weights(step)
        products = [dot(gained, held[which]) for which in range(3)]
        totals = products if totals is None else [t + p for t, p in zip(totals, products)]
    return totals, squares


def qkv_early(places, kept_masks, count, *refs):
    blocks, (gain_ref, w_ref, kept_ref, totals_ref, squares_ref, held, sems) = (
        refs[:count],
        refs[count:],
    )
    order = list(places)
    streamed = [m for m in order if m not in kept_masks]
    copies = start_all(
        [slice_copy(w_ref, m, held.at[n], sems.at[n]) for n, m in enumerate(streamed)]
    )

    def weights(step):
        mask = order[step]
        if mask in kept_masks:
            return kept_ref.at[kept_masks.index(mask)]
        copies[streamed.index(mask)].wait()
        return held.at[streamed.index(mask)]

    totals, squares = qkv_steps(places, blocks, gain_ref, weights, None, None)
    for which in range(3):
        totals_ref[which] = totals[which]
    squares_ref[...] = jnp.broadcast_to(squares, squares_ref.shape)


def qkv_late(places, features, count, *refs):
    blocks = refs[:count]
    gain_ref, kept_ref, totals_ref, squares_ref, q_ref, kv_ref = refs[count:]
    totals, squares = qkv_steps(
        places,
        blocks,
        gain_ref,
        lambda step: kept_ref.at[step],
        [totals_ref[which] for which in range(3)],
        squares_ref[:, :1],
    )
    scale = lax.rsqrt(squares / features + epsilon)
    q_ref[...] = (totals[0] * scale).astype(jnp.bfloat16)
    kv_ref[0] = (totals[1] * scale).astype(jnp.bfloat16)
    kv_ref[1] = (totals[2] * scale).astype(jnp.bfloat16)


def write_chunks(plan, attended_ref, w_ref, out_refs):
    columns = attended_ref.shape[1]
    for mask in dict.fromkeys(m for _, parts, _ in plan for m, _, _ in parts):
        chunk = dot(attended_ref[...], w_ref[:, pl.ds(offset(mask, columns), columns)])
        write_parts(plan, mask, lambda first, last: chunk[first:last], out_refs, slice(None))


def write_parts(plan, mask, rows, out_refs, columns):
    for (_, parts, _), ref in zip(plan, out_refs):
        at = 0
        for m, first, last in parts:
            if m == mask:
                ref[at : at + last - first, columns] = rows(first, last).astype(ref.dtype)
            at += last - first


def attend_kernel(plan, q_ref, own_ref, other_ref, w_ref, attended_ref, *out_refs):
    columns = q_ref.shape[1]
    contract = (((1,), (1,)), ((), ()))
    for head in range(columns // HD):
        here = slice(head * HD, (head + 1) * HD)
        query = q_ref[:, here]
        scores = [
            lax.dot_general(query, kv[0, :, here], contract, preferred_element_type=jnp.float32)
            * (1.0 / math.sqrt(HD))
            for kv in (own_ref, other_ref)
        ]
        peak = jnp.maximum(*[jnp.max(s, axis=1, keepdims=True) for s in scores])
        weights = [jnp.exp(s - peak) for s in scores]
        norm = sum(jnp.sum(w, axis=1, keepdims=True) for w in weights)
        attended_ref[:, here] = sum(
            dot((w / norm).astype(jnp.bfloat16), kv[1, :, here])
            for w, kv in zip(weights, (own_ref, other_ref))
        ).astype(jnp.bfloat16)
    write_chunks(plan, attended_ref, w_ref, out_refs)


def out_kernel(plan, attended_ref, w_ref, *out_refs):
    write_chunks(plan, attended_ref, w_ref, out_refs)


def up_kernel(size, plan, places, pieces, coarse_ref, own_ref, *refs):
    count = len(places)
    arrived, w_ref, out_refs, (mixed_ref, sums) = (
        refs[:count],
        refs[count],
        refs[count + 1 : -2],
        refs[-2:],
    )
    width = w_ref.shape[1] // pieces
    mixed_ref[...] = own_ref[...]
    for value, (source, target, rows) in zip(arrived, places):
        mixed_ref[target : target + rows, :] += value[source : source + rows].astype(jnp.float32)
    mixed = (coarse_ref[...].astype(jnp.float32) + mixed_ref[...]).astype(jnp.bfloat16)
    own_tokens = mixed.shape[0] // size
    for p in range(pieces):
        here = slice(p * width, (p + 1) * width)
        sums[...] = dot(mixed, w_ref[:, here])
        for mask in range(size):
            chunk = sums[pl.ds(offset(mask, own_tokens), own_tokens), :]
            write_parts(plan, mask, lambda first, last: chunk[first:last], out_refs, here)


def scaled(rows, gain):
    mean = jnp.mean(rows * rows, axis=1, keepdims=True)
    return (rows * lax.rsqrt(mean + epsilon) * gain).astype(jnp.bfloat16).astype(jnp.float32)


def norm_kernel(frames_ref, gain_ref, taps_ref, normed_ref, kept_ref, wide_ref, held, taps, sems):
    copies = start_all(
        [
            pltpu.make_async_copy(source, target, sems.at[n])
            for n, (source, target) in enumerate(
                [(frames_ref, held), (gain_ref, kept_ref), (taps_ref, taps)]
            )
        ]
    )
    for copy in copies:
        copy.wait()
    wide_ref[...] = taps[...].astype(jnp.float32)
    normed_ref[...] = scaled(held[...].astype(jnp.float32), kept_ref[...])


def conv_kernel(before_ref, after_ref, normed_ref, gain_ref, taps_ref, out_ref, padded):
    frame_rows = normed_ref.shape[0]
    edge = KW // 2
    padded[8 - edge : 8, :] = scaled(before_ref[...].astype(jnp.float32), gain_ref[...])
    padded[8 : 8 + frame_rows, :] = normed_ref[...]
    padded[8 + frame_rows : 8 + frame_rows + edge, :] = scaled(
        after_ref[...].astype(jnp.float32), gain_ref[...]
    )
    total = None
    for tap in range(KW):
        first = 8 - edge + tap
        part = padded[first : first + frame_rows, :] * taps_ref[tap : tap + 1, :]
        total = part if total is None else total + part
    out_ref[...] = total.astype(jnp.bfloat16)


def edge_rows(frames, width):
    size, inner = lax.axis_size("seq"), lax.axis_size("sub")
    position = lax.axis_index("seq") * inner + lax.axis_index("sub")
    total = size * inner
    first, last = frames[:width], frames[-width:]
    even = (position & 1) == 0
    inside = [(i, i ^ 1) for i in range(total)]
    across = [(i, ((i + 1) ^ 1) - 1) for i in range(1, total - 1)]
    near = lax.ppermute(jnp.where(even, last, first), ("seq", "sub"), inside)
    far = lax.ppermute(jnp.where(even, first, last), ("seq", "sub"), across)
    return jnp.where(even, far, near), jnp.where(even, near, far)


def per_device(frames, fine_gain, dw_kernel, w_down, coarse_gain, w_qkv, w_out, w_up):
    frame_rows = frames.shape[0]
    columns = w_qkv.shape[2]
    size = lax.axis_size("seq")
    features = columns * size
    own_tokens = frame_rows // 4
    tokens = own_tokens * size
    bf16, f32 = jnp.bfloat16, jnp.float32

    before, after = edge_rows(frames, KW // 2)
    frames_f32 = frames.astype(f32)

    normed, gain_kept, taps = call(
        norm_kernel,
        (sds(frames.shape, f32), sds((1, DF), f32), sds(dw_kernel.shape, f32)),
        [VMEM(frames.shape, bf16), VMEM(dw_kernel.shape, bf16), pltpu.SemaphoreType.DMA((3,))],
        "hhh",
        frames,
        fine_gain.reshape(1, DF),
        dw_kernel,
    )
    patches = call(
        conv_kernel,
        sds(frames.shape, bf16),
        [VMEM((frame_rows + 16, DF), f32)],
        "vvvvv",
        before,
        after,
        normed,
        gain_kept,
        taps,
    ).reshape(own_tokens, 4 * DF)

    pieces = 8
    early, late = early_masks(size), late_masks(size)

    w_down_kept, w_out_kept = fetch(patches, w_down, w_out)
    arrays, places = gather_flips(patches, "seq", (w_down_kept, w_out_kept))
    which, here = needed(places, early)
    coarse, w_up_kept = call(
        functools.partial(down_early, here, len(which)),
        (sds((tokens, columns), bf16), sds(w_up.shape, bf16)),
        [pltpu.SemaphoreType.DMA],
        "v" * len(which) + "vh",
        *[arrays[i] for i in which],
        w_down_kept,
        w_up,
    )
    which, here = needed(places, late)
    coarse = call(
        functools.partial(down_late, here, len(which)),
        sds((tokens, columns), bf16),
        [],
        "v" * len(which) + "vv",
        *[arrays[i] for i in which],
        w_down_kept,
        coarse,
        aliases={len(which) + 1: 0},
    )

    kept_masks = late + early[: len(early) // 2]
    streamed = [m for m in early if m not in kept_masks]
    kept = call(
        functools.partial(fetch_slices_kernel, kept_masks),
        sds((len(kept_masks), 3, columns, columns), bf16),
        [pltpu.SemaphoreType.DMA((len(kept_masks),))],
        "hv",
        w_qkv,
        coarse,
    )
    arrays, places = gather_flips(coarse, "seq", (kept,))
    gain_row = coarse_gain.reshape(1, features)
    which, here = needed(places, early)
    totals, squares = call(
        functools.partial(qkv_early, here, kept_masks, len(which)),
        (sds((3, tokens, columns), f32), sds((tokens, 128), f32)),
        [
            VMEM((len(streamed), 3, columns, columns), bf16),
            pltpu.SemaphoreType.DMA((len(streamed),)),
        ],
        "v" * len(which) + "vhv",
        *[arrays[i] for i in which],
        gain_row,
        w_qkv,
        kept,
    )
    which, here = needed(places, late)
    queries, own_kv = call(
        functools.partial(qkv_late, here, features, len(which)),
        (sds((tokens, columns), bf16), sds((2, tokens, columns), bf16)),
        [],
        "v" * len(which) + "vvvv",
        *[arrays[i] for i in which],
        gain_row,
        kept,
        totals,
        squares,
    )
    other_kv = flip(own_kv, "sub", 1)

    def planned(plan, width):
        return tuple(
            sds((sum(last - first for _, first, last in parts), width), f32 if wide else bf16)
            for _, parts, wide in plan
        )

    first_plan, second_plan = scatter_plan(size, tokens)
    attended, *first = call(
        functools.partial(attend_kernel, first_plan),
        (sds((tokens, columns), bf16),) + planned(first_plan, columns),
        [],
        "vvvv",
        queries,
        own_kv,
        other_kv,
        w_out_kept,
    )
    second = call(
        functools.partial(out_kernel, second_plan),
        planned(second_plan, columns),
        [],
        "vv",
        attended,
        w_out_kept,
    )
    names = [name for name, _, _ in first_plan + second_plan]
    parts = dict(zip(names, [*first, *second]))
    arrived = scatter_flips(parts, "seq")[::-1]
    first_plan, second_plan = scatter_plan(size, own_tokens)
    lifted = call(
        functools.partial(
            up_kernel, size, first_plan + second_plan, [a[1:] for a in arrived], pieces
        ),
        planned(first_plan + second_plan, 4 * DF),
        [VMEM((tokens, columns), f32), VMEM((tokens, 4 * DF // pieces), f32)],
        "vv" + "v" * len(arrived) + "v",
        coarse,
        parts["own"],
        *[a[0] for a in arrived],
        w_up_kept,
    )
    parts = dict(zip(names, lifted))
    total = parts["own"]
    for value, source, target, rows in scatter_flips(parts, "seq"):
        value = value[source : source + rows].astype(f32)
        total = total + jnp.pad(value, ((target, own_tokens - target - rows), (0, 0)))
    return (frames_f32 + total.reshape(frame_rows, DF)).astype(bf16)


def solution(mesh):
    placed = (
        P(("groups", "seq", "sub"), None),
        P(),
        P(),
        P(None, "seq"),
        P(),
        P(None, None, "seq"),
        P("seq", None),
        P("seq", None),
    )
    return jax.shard_map(
        per_device,
        mesh=mesh,
        in_specs=placed,
        out_specs=P(("groups", "seq", "sub"), None),
        check_vma=False,
    )
```

```python
import functools
import math

import jax
import jax.numpy as jnp
from jax import lax
from jax.experimental import pallas as pl
from jax.experimental.pallas import tpu as pltpu
from jax.sharding import PartitionSpec as P

DF = 1024
HD = 128
KW = 5
VMEM = pltpu.VMEM


epsilon = 1e-06


def flip(value, axis, mask):
    pairs = [(source, source ^ mask) for source in range(lax.axis_size(axis))]
    return lax.ppermute(value, axis, pairs)


def relayed(mask, size):
    return mask & 1 == 1 and mask >= max(size // 2, 2)


def far_first(size):
    return sorted(range(1, size), reverse=True)


def after_all(values, others):
    return lax.optimization_barrier((tuple(values), tuple(others)))[0]


def gather_flips(value, axis, fetched):
    size, rows = lax.axis_size(axis), value.shape[0]
    arrays = [value] + [None] * (size - 1)
    for mask in far_first(size):
        if not relayed(mask, size):
            arrays[mask] = flip(value, axis, mask)
    near = [arrays[m] for m in range(1, size) if arrays[m] is not None and m == 3]
    for n, mask in enumerate(m for m in far_first(size) if relayed(m, size)):
        ready = (*fetched, *near) if n else fetched
        arrays[mask] = flip(after_all((arrays[mask ^ 1],), ready)[0], axis, 1)
    return arrays, {mask: [(mask, 0, rows)] for mask in range(size)}


def late_masks(size):
    return [m for m in range(size) if relayed(m, size)]


def early_masks(size):
    return [m for m in range(size) if m not in late_masks(size)]


def scatter_plan(size, rows):
    relays = [m for m in far_first(size) if relayed(m, size)]
    via = [m ^ 1 for m in relays]
    rest = via + [m for m in far_first(size) if m not in via and m not in relays]
    first = [(m, [(m, 0, rows)], False) for m in relays]
    second = [(m, [(m, 0, rows)], m in via) for m in rest] + [("own", [(0, 0, rows)], True)]
    return first, second


def scatter_flips(parts, axis):
    size, rows = lax.axis_size(axis), parts["own"].shape[0]

    def plus(part, *others):
        return sum([o.astype(jnp.float32) for o in others], part).astype(jnp.bfloat16)

    passed = {m ^ 1: flip(parts[m], axis, 1) for m in far_first(size) if relayed(m, size)}
    beside = flip(parts[2], axis, 2)
    arrived = [(beside, 0, 0, rows)]
    for mask in far_first(size):
        if mask in passed:
            part = plus(parts[mask], passed[mask])
        elif mask == 2 or relayed(mask, size):
            continue
        else:
            part = after_all((parts[mask],), (beside, *passed.values()))[0]
        arrived.append((flip(part, axis, mask), 0, 0, rows))
    return arrived


def call(body, outs, scratch, in_memory, *operands, aliases=None):
    specs = [
        pl.BlockSpec(memory_space=pl.ANY if where == "h" else VMEM) for where in in_memory
    ]
    return pl.pallas_call(
        body,
        out_shape=outs,
        in_specs=specs,
        out_specs=jax.tree.map(lambda _: pl.BlockSpec(memory_space=VMEM), outs),
        scratch_shapes=scratch,
        input_output_aliases=aliases or {},
        compiler_params=pltpu.CompilerParams(vmem_limit_bytes=20 * 2**20),
    )(
        *[
            pltpu.with_memory_space_constraint(o, pltpu.HBM) if where == "h" else o
            for where, o in zip(in_memory, operands)
        ]
    )


def sds(shape, dtype):
    return jax.ShapeDtypeStruct(shape, dtype)


def dot(left, right):
    return jnp.dot(left, right, preferred_element_type=jnp.float32)


def offset(mask, width):
    return pl.multiple_of((lax.axis_index("seq") ^ mask) * width, width)


def start_all(copies):
    for copy in copies:
        copy.start()
    return copies


def rows_of(refs, place):
    parts = [refs[i][first : first + rows] for i, first, rows in place]
    return parts[0] if len(parts) == 1 else jnp.concatenate(parts, axis=0)


def needed(places, masks):
    which = sorted({i for mask in masks for i, _, _ in places[mask]})
    number = {i: n for n, i in enumerate(which)}
    return which, {m: [(number[i], f, r) for i, f, r in places[m]] for m in masks}


def down_rows(places, refs, product, out_ref):
    first = 0
    for mask, place in places.items():
        rows = sum(r for _, _, r in place)
        out_ref[pl.ds(offset(mask, rows), rows), :] = product[first : first + rows].astype(
            jnp.bfloat16
        )
        first += rows


def fetch_kernel(count, *refs):
    sources, targets, sems = refs[:count], refs[count + 1 : -1], refs[-1]
    copies = start_all(
        [
            pltpu.make_async_copy(source, target, sems.at[n])
            for n, (source, target) in enumerate(zip(sources, targets))
        ]
    )
    for copy in copies:
        copy.wait()


def fetch(after, *weights):
    count = len(weights)
    return call(
        functools.partial(fetch_kernel, count),
        tuple(sds(w.shape, w.dtype) for w in weights),
        [pltpu.SemaphoreType.DMA((count,))],
        "h" * count + "v",
        *weights,
        after,
    )


def slice_copy(w_ref, mask, target, sem):
    columns = target.shape[1]
    return pltpu.make_async_copy(
        w_ref.at[:, pl.ds(offset(mask, columns), columns), :], target, sem
    )


def fetch_slices_kernel(masks, w_ref, _, kept_ref, sems):
    copies = start_all(
        [slice_copy(w_ref, m, kept_ref.at[n], sems.at[n]) for n, m in enumerate(masks)]
    )
    for copy in copies:
        copy.wait()


def down_early(places, count, *refs):
    blocks, (w_ref, later_ref, out_ref, kept_ref, sem) = refs[:count], refs[count:]
    copy = pltpu.make_async_copy(later_ref, kept_ref, sem)
    copy.start()
    rows = jnp.concatenate([rows_of(blocks, place) for place in places.values()], axis=0)
    down_rows(places, blocks, dot(rows, w_ref[...]), out_ref)
    copy.wait()


def down_late(places, count, *refs):
    blocks, w_ref, _, out_ref = refs[:count], *refs[count:]
    rows = jnp.concatenate([rows_of(blocks, place) for place in places.values()], axis=0)
    down_rows(places, blocks, dot(rows, w_ref[...]), out_ref)


def qkv_steps(places, blocks, gain_ref, weights, totals, squares):
    for step, (mask, place) in enumerate(places.items()):
        block = rows_of(blocks, place).astype(jnp.float32)
        columns = block.shape[1]
        part = jnp.sum(block * block, axis=1, keepdims=True)
        squares = part if squares is None else squares + part
        gained = (block * gain_ref[:, pl.ds(offset(mask, columns), columns)]).astype(jnp.bfloat16)
        held = weights(step)
        products = [dot(gained, held[which]) for which in range(3)]
        totals = products if totals is None else [t + p for t, p in zip(totals, products)]
    return totals, squares


def qkv_early(places, kept_masks, count, *refs):
    blocks, (gain_ref, w_ref, kept_ref, totals_ref, squares_ref, held, sems) = (
        refs[:count],
        refs[count:],
    )
    order = list(places)
    streamed = [m for m in order if m not in kept_masks]
    copies = start_all(
        [slice_copy(w_ref, m, held.at[n], sems.at[n]) for n, m in enumerate(streamed)]
    )

    def weights(step):
        mask = order[step]
        if mask in kept_masks:
            return kept_ref.at[kept_masks.index(mask)]
        copies[streamed.index(mask)].wait()
        return held.at[streamed.index(mask)]

    totals, squares = qkv_steps(places, blocks, gain_ref, weights, None, None)
    for which in range(3):
        totals_ref[which] = totals[which]
    squares_ref[...] = jnp.broadcast_to(squares, squares_ref.shape)


def qkv_late(places, features, count, *refs):
    blocks = refs[:count]
    gain_ref, kept_ref, totals_ref, squares_ref, q_ref, kv_ref = refs[count:]
    totals, squares = qkv_steps(
        places,
        blocks,
        gain_ref,
        lambda step: kept_ref.at[step],
        [totals_ref[which] for which in range(3)],
        squares_ref[:, :1],
    )
    scale = lax.rsqrt(squares / features + epsilon)
    q_ref[...] = (totals[0] * scale).astype(jnp.bfloat16)
    kv_ref[0] = (totals[1] * scale).astype(jnp.bfloat16)
    kv_ref[1] = (totals[2] * scale).astype(jnp.bfloat16)


def write_chunks(plan, attended_ref, w_ref, out_refs):
    columns = attended_ref.shape[1]
    for mask in dict.fromkeys(m for _, parts, _ in plan for m, _, _ in parts):
        chunk = dot(attended_ref[...], w_ref[:, pl.ds(offset(mask, columns), columns)])
        write_parts(plan, mask, lambda first, last: chunk[first:last], out_refs, slice(None))


def write_parts(plan, mask, rows, out_refs, columns):
    for (_, parts, _), ref in zip(plan, out_refs):
        at = 0
        for m, first, last in parts:
            if m == mask:
                ref[at : at + last - first, columns] = rows(first, last).astype(ref.dtype)
            at += last - first


def head_scores(query, keys):
    return lax.dot_general(
        query, keys, (((1,), (1,)), ((), ())), preferred_element_type=jnp.float32
    ) * (1.0 / math.sqrt(HD))


def own_scores_kernel(q_ref, own_ref, scores_ref):
    for head in range(scores_ref.shape[0]):
        here = slice(head * HD, (head + 1) * HD)
        scores_ref[head] = head_scores(q_ref[:, here], own_ref[0, :, here])


def attend_kernel(
    plan, q_ref, scores_ref, own_ref, other_ref, w_ref, attended_ref, *out_refs
):
    columns = q_ref.shape[1]
    for head in range(columns // HD):
        here = slice(head * HD, (head + 1) * HD)
        scores = [scores_ref[head], head_scores(q_ref[:, here], other_ref[0, :, here])]
        peak = jnp.maximum(*[jnp.max(s, axis=1, keepdims=True) for s in scores])
        weights = [jnp.exp(s - peak) for s in scores]
        norm = sum(jnp.sum(w, axis=1, keepdims=True) for w in weights)
        mixed = sum(
            dot(w.astype(jnp.bfloat16), kv[1, :, here])
            for w, kv in zip(weights, (own_ref, other_ref))
        )
        attended_ref[:, here] = (mixed * (1.0 / norm)).astype(jnp.bfloat16)
    write_chunks(plan, attended_ref, w_ref, out_refs)


def out_kernel(plan, attended_ref, w_ref, *out_refs):
    write_chunks(plan, attended_ref, w_ref, out_refs)


def up_kernel(size, plan, places, pieces, coarse_ref, own_ref, *refs):
    count = len(places)
    arrived, w_ref, out_refs, (mixed_ref, sums) = (
        refs[:count],
        refs[count],
        refs[count + 1 : -2],
        refs[-2:],
    )
    width = w_ref.shape[1] // pieces
    mixed_ref[...] = own_ref[...]
    for value, (source, target, rows) in zip(arrived, places):
        mixed_ref[target : target + rows, :] += value[source : source + rows].astype(jnp.float32)
    mixed = (coarse_ref[...].astype(jnp.float32) + mixed_ref[...]).astype(jnp.bfloat16)
    own_tokens = mixed.shape[0] // size
    for p in range(pieces):
        here = slice(p * width, (p + 1) * width)
        sums[...] = dot(mixed, w_ref[:, here])
        for mask in range(size):
            chunk = sums[pl.ds(offset(mask, own_tokens), own_tokens), :]
            write_parts(plan, mask, lambda first, last: chunk[first:last], out_refs, here)


def scaled(rows, gain):
    mean = jnp.mean(rows * rows, axis=1, keepdims=True)
    return (rows * lax.rsqrt(mean + epsilon) * gain).astype(jnp.bfloat16).astype(jnp.float32)


def norm_kernel(frames_ref, gain_ref, taps_ref, normed_ref, kept_ref, wide_ref, held, taps, sems):
    copies = start_all(
        [
            pltpu.make_async_copy(source, target, sems.at[n])
            for n, (source, target) in enumerate(
                [(frames_ref, held), (gain_ref, kept_ref), (taps_ref, taps)]
            )
        ]
    )
    for copy in copies:
        copy.wait()
    wide_ref[...] = taps[...].astype(jnp.float32)
    normed_ref[...] = scaled(held[...].astype(jnp.float32), kept_ref[...])


def conv_kernel(before_ref, after_ref, normed_ref, gain_ref, taps_ref, out_ref, padded):
    frame_rows = normed_ref.shape[0]
    edge = KW // 2
    padded[8 - edge : 8, :] = scaled(before_ref[...].astype(jnp.float32), gain_ref[...])
    padded[8 : 8 + frame_rows, :] = normed_ref[...]
    padded[8 + frame_rows : 8 + frame_rows + edge, :] = scaled(
        after_ref[...].astype(jnp.float32), gain_ref[...]
    )
    total = None
    for tap in range(KW):
        first = 8 - edge + tap
        part = padded[first : first + frame_rows, :] * taps_ref[tap : tap + 1, :]
        total = part if total is None else total + part
    out_ref[...] = total.astype(jnp.bfloat16)


def edge_rows(frames, width):
    size, inner = lax.axis_size("seq"), lax.axis_size("sub")
    position = lax.axis_index("seq") * inner + lax.axis_index("sub")
    total = size * inner
    first, last = frames[:width], frames[-width:]
    even = (position & 1) == 0
    inside = [(i, i ^ 1) for i in range(total)]
    across = [(i, ((i + 1) ^ 1) - 1) for i in range(1, total - 1)]
    near = lax.ppermute(jnp.where(even, last, first), ("seq", "sub"), inside)
    far = lax.ppermute(jnp.where(even, first, last), ("seq", "sub"), across)
    return jnp.where(even, far, near), jnp.where(even, near, far)


def per_device(frames, fine_gain, dw_kernel, w_down, coarse_gain, w_qkv, w_out, w_up):
    frame_rows = frames.shape[0]
    columns = w_qkv.shape[2]
    size = lax.axis_size("seq")
    features = columns * size
    own_tokens = frame_rows // 4
    tokens = own_tokens * size
    bf16, f32 = jnp.bfloat16, jnp.float32

    before, after = edge_rows(frames, KW // 2)
    frames_f32 = frames.astype(f32)

    normed, gain_kept, taps = call(
        norm_kernel,
        (sds(frames.shape, f32), sds((1, DF), f32), sds(dw_kernel.shape, f32)),
        [VMEM(frames.shape, bf16), VMEM(dw_kernel.shape, bf16), pltpu.SemaphoreType.DMA((3,))],
        "hhh",
        frames,
        fine_gain.reshape(1, DF),
        dw_kernel,
    )
    patches = call(
        conv_kernel,
        sds(frames.shape, bf16),
        [VMEM((frame_rows + 16, DF), f32)],
        "vvvvv",
        before,
        after,
        normed,
        gain_kept,
        taps,
    ).reshape(own_tokens, 4 * DF)

    pieces = 8
    early, late = early_masks(size), late_masks(size)

    w_down_kept, w_out_kept = fetch(patches, w_down, w_out)
    arrays, places = gather_flips(patches, "seq", (w_down_kept, w_out_kept))
    which, here = needed(places, early)
    coarse, w_up_kept = call(
        functools.partial(down_early, here, len(which)),
        (sds((tokens, columns), bf16), sds(w_up.shape, bf16)),
        [pltpu.SemaphoreType.DMA],
        "v" * len(which) + "vh",
        *[arrays[i] for i in which],
        w_down_kept,
        w_up,
    )
    which, here = needed(places, late)
    coarse = call(
        functools.partial(down_late, here, len(which)),
        sds((tokens, columns), bf16),
        [],
        "v" * len(which) + "vv",
        *[arrays[i] for i in which],
        w_down_kept,
        coarse,
        aliases={len(which) + 1: 0},
    )

    kept_masks = late + early[: len(early) // 2]
    streamed = [m for m in early if m not in kept_masks]
    kept = call(
        functools.partial(fetch_slices_kernel, kept_masks),
        sds((len(kept_masks), 3, columns, columns), bf16),
        [pltpu.SemaphoreType.DMA((len(kept_masks),))],
        "hv",
        w_qkv,
        coarse,
    )
    arrays, places = gather_flips(coarse, "seq", (kept,))
    gain_row = coarse_gain.reshape(1, features)
    which, here = needed(places, early)
    totals, squares = call(
        functools.partial(qkv_early, here, kept_masks, len(which)),
        (sds((3, tokens, columns), f32), sds((tokens, 128), f32)),
        [
            VMEM((len(streamed), 3, columns, columns), bf16),
            pltpu.SemaphoreType.DMA((len(streamed),)),
        ],
        "v" * len(which) + "vhv",
        *[arrays[i] for i in which],
        gain_row,
        w_qkv,
        kept,
    )
    which, here = needed(places, late)
    queries, own_kv = call(
        functools.partial(qkv_late, here, features, len(which)),
        (sds((tokens, columns), bf16), sds((2, tokens, columns), bf16)),
        [],
        "v" * len(which) + "vvvv",
        *[arrays[i] for i in which],
        gain_row,
        kept,
        totals,
        squares,
    )
    other_kv = flip(own_kv, "sub", 1)
    own_scores = call(
        own_scores_kernel,
        sds((columns // HD, tokens, tokens), f32),
        [],
        "vv",
        queries,
        own_kv,
    )

    def planned(plan, width):
        return tuple(
            sds((sum(last - first for _, first, last in parts), width), f32 if wide else bf16)
            for _, parts, wide in plan
        )

    first_plan, second_plan = scatter_plan(size, tokens)
    attended, *first = call(
        functools.partial(attend_kernel, first_plan),
        (sds((tokens, columns), bf16),) + planned(first_plan, columns),
        [],
        "vvvvv",
        queries,
        own_scores,
        own_kv,
        other_kv,
        w_out_kept,
    )
    second = call(
        functools.partial(out_kernel, second_plan),
        planned(second_plan, columns),
        [],
        "vv",
        attended,
        w_out_kept,
    )
    names = [name for name, _, _ in first_plan + second_plan]
    parts = dict(zip(names, [*first, *second]))
    arrived = scatter_flips(parts, "seq")[::-1]
    first_plan, second_plan = scatter_plan(size, own_tokens)
    lifted = call(
        functools.partial(
            up_kernel, size, first_plan + second_plan, [a[1:] for a in arrived], pieces
        ),
        planned(first_plan + second_plan, 4 * DF),
        [VMEM((tokens, columns), f32), VMEM((tokens, 4 * DF // pieces), f32)],
        "vv" + "v" * len(arrived) + "v",
        coarse,
        parts["own"],
        *[a[0] for a in arrived],
        w_up_kept,
    )
    parts = dict(zip(names, lifted))
    total = parts["own"]
    for value, source, target, rows in scatter_flips(parts, "seq"):
        value = value[source : source + rows].astype(f32)
        total = total + jnp.pad(value, ((target, own_tokens - target - rows), (0, 0)))
    return (frames_f32 + total.reshape(frame_rows, DF)).astype(bf16)


def solution(mesh):
    placed = (
        P(("groups", "seq", "sub"), None),
        P(),
        P(),
        P(None, "seq"),
        P(),
        P(None, None, "seq"),
        P("seq", None),
        P("seq", None),
    )
    return jax.shard_map(
        per_device,
        mesh=mesh,
        in_specs=placed,
        out_specs=P(("groups", "seq", "sub"), None),
        check_vma=False,
    )
```
